32 devices in a mesh: gx: 4 (over y, core), gy: 8 (over z, x).
Axes of the slice: x: 2, y: 2, z: 4, core: 2. Of those that a mesh axis runs over, the one named last changes fastest.
Arguments:
- row_ids: int32 [65536], P(('gx', 'gy')), may hold values from 0 to 262143, as said below
- block_map: int32 [2048], replicated, may hold values from 0 to 2047, as said below
- grad_tiles: float32 [65536, 128], P(('gx', 'gy')), may hold values from -6 to 6
- table: float32 [262144, 128], P(('gx', 'gy')), may hold values from -4 to 4
- accum: float32 [262144], P(('gx', 'gy')), may hold values from 0.05 to 2
Outputs:
- new_table: float32 [262144, 128], P(('gx', 'gy'))
- new_accum: float32 [262144], P(('gx', 'gy'))
The draws below stay inside these ranges and needn't reach their ends.
Inputs may be any that keep to these rules, and one draw needn't show every extreme that they name: `row_ids`: storage position p lies on device p // 8192 of the gx+gy order. Among the lookups of one device, at most 128 have positions on any one device; in every draw one device holds exactly 128 positions of the lookups of every device. Rows repeat within and across devices. `block_map`: each number appears once.
All inputs are finite; a program needn't handle non-finite values.
Results may differ from the reference program's by a relative error of at most 0.00002.
Values sent between devices are 32-bit elements; how exact they have to be, the bound alone decides.
No kernel may reach another device: no remote copies, remote signals or barrier semaphores. Data moves between devices by JAX's collectives and lax.ppermute only.
A program may use at most 64 MiB of HBM per device.

```python
import math
import jax
import jax.numpy as jnp
from jax import lax

E = 128
ROWS_DEV = 8192
LOOK_DEV = 2048
BLOCK = 128
CAP = 128
ROWS = 262144
BLOCKS = 2048
LOOKUPS = 65536
DEVICES = 32


def route_layout(key):
    base_key = jax.random.fold_in(key, 4242)
    streams = jax.random.split(base_key, 8)
    block_map = jax.random.permutation(streams[0], BLOCKS).astype(jnp.int32)
    inverse = jnp.zeros((BLOCKS,), jnp.int32).at[block_map].set(jnp.arange(BLOCKS, dtype=jnp.int32))
    hot_owner = jax.random.randint(streams[1], (), 0, DEVICES).astype(jnp.int32)
    sources = jnp.arange((DEVICES - 1) * CAP, dtype=jnp.int32) // CAP
    sources = sources + (sources >= hot_owner).astype(jnp.int32)
    device_keys = jax.random.split(streams[2], DEVICES)
    spread = jax.vmap(lambda k: jax.random.permutation(k, sources)[:LOOK_DEV - CAP])(device_keys)
    owners = jnp.concatenate([jnp.full((DEVICES, CAP), hot_owner, jnp.int32), spread], axis=1)
    shuffle_keys = jax.random.split(streams[3], DEVICES)
    owners = jax.vmap(lambda k, v: jax.random.permutation(k, v))(shuffle_keys, owners)
    hot_slots = jax.random.randint(streams[4], (16,), 0, ROWS_DEV).astype(jnp.int32)
    chosen = jax.random.randint(streams[5], (DEVICES, LOOK_DEV), 0, 16)
    choose = jax.random.randint(streams[6], (DEVICES, LOOK_DEV), 0, 2)
    spread_slots = jax.random.randint(streams[7], (DEVICES, LOOK_DEV), 0, ROWS_DEV).astype(jnp.int32)
    slot_ids = jnp.where(choose == 0, hot_slots[chosen], spread_slots)
    position = owners * ROWS_DEV + slot_ids
    row_index = inverse[position // BLOCK] * BLOCK + position % BLOCK
    return (block_map, row_index.reshape(-1).astype(jnp.int32))


def draw_row_ids(key, part):
    return route_layout(key)[1]


def draw_block_map(key, part):
    return route_layout(key)[0]


def steps_of(own_key, dims, shards, least, largest):
    level = 1.0
    for dim, blocks in shards:
        steps = jax.random.uniform(jax.random.fold_in(jax.random.fold_in(own_key, 6), dim), (blocks,), jnp.float32, least / len(shards), largest / len(shards))
        level = level * jnp.repeat(jnp.exp(steps), dims[dim] // blocks).reshape((-1,) + (1,) * (len(dims) - 1 - dim))
    return level


def noise(key, shape, scale, bound, cuts=(), kind=jnp.bfloat16):
    entries = scale * jax.random.normal(key, shape, jnp.float32)
    if cuts:
        entries = entries * steps_of(key, shape, cuts, -0.22, 0.18)
    return jnp.clip(entries, -bound, bound).astype(kind)


def setup_inputs(seed: int = 0) -> dict:
    key_of = jax.random.split(jax.random.key(seed), 6)
    row_ids = draw_row_ids(jax.random.fold_in(key_of[5], 71), 0)
    block_map = draw_block_map(jax.random.fold_in(key_of[5], 71), 0)
    grad_tiles = noise(key_of[2], (LOOKUPS, E), 1.0, 6.0, ((0, 32),), jnp.float32)
    table = noise(key_of[3], (ROWS, E), 0.5, 4.0, ((0, 32),), jnp.float32)
    accum = jnp.clip(jnp.exp(math.log(2.0) - 3.6888794 * jax.random.uniform(key_of[4], (ROWS,), jnp.float32) ** steps_of(key_of[4], (ROWS,), ((0, 32),), -0.2, 0.2)), 0.05, 2.0)
    return {"row_ids": row_ids, "block_map": block_map, "grad_tiles": grad_tiles, "table": table, "accum": accum}


learning_rate = 0.25
epsilon = 1e-08

def reference(row_ids, block_map, grad_tiles, table, accum):
    position = (jnp.take(block_map, row_ids // BLOCK) * BLOCK + row_ids % BLOCK).astype(jnp.int32)
    row_grad = jax.ops.segment_sum(grad_tiles, position, num_segments=ROWS)
    new_accum = accum + lax.optimization_barrier(jnp.mean(row_grad * row_grad, axis=1))
    new_table = table - learning_rate * row_grad / (jnp.sqrt(new_accum) + epsilon)[:, None]
    return (new_table, new_accum)
```

```python
import functools

import jax
import jax.numpy as jnp
from jax import lax
from jax.experimental import pallas as pl
from jax.experimental.pallas import tpu as pltpu
from jax.sharding import PartitionSpec as P

BLOCK = 128
LANES = 128
STREAMS = 4
UNROLL = 16
CHUNKS = 8

learning_rate = 0.25
epsilon = 1e-08


def split(x, n):
    if n & (n - 1) == 0:
        return lax.shift_right_logical(x, n.bit_length() - 1), x & (n - 1)
    return lax.div(x, n), lax.rem(x, n)


def bin_kernel(
    devices, rows_dev, ids_ref, map_ref, grad_hbm, send_ref, info_ref, grad_ref, cols, marks, target_vmem, target, sums, sems
):
    blocks = ids_ref.shape[0]
    width = send_ref.shape[0] // devices
    slots = width - 1
    drop = devices * width
    fetch = pltpu.make_async_copy(grad_hbm, grad_ref, sems.at[0])
    fetch.start()

    block, within = split(ids_ref[...], BLOCK)
    high, low = split(block, LANES)
    mapped = jnp.zeros_like(block)
    for h in range(map_ref.shape[0]):
        row = jnp.broadcast_to(map_ref[h : h + 1, :], low.shape)
        mapped = jnp.where(high == h, jnp.take_along_axis(row, low, axis=1), mapped)
    position = mapped * BLOCK + within
    owner, slot = split(position, rows_dev)

    def column(row):
        return jnp.transpose(jnp.broadcast_to(row, (LANES, LANES)))

    for b in range(blocks):
        cols[b * LANES : (b + 1) * LANES, :] = column(position[b : b + 1, :])
    rows = [jnp.broadcast_to(position[b : b + 1, :], (8, LANES)) for b in range(blocks)]
    per_block = LANES // 8
    none = blocks * per_block
    first = [jnp.full((8, LANES), none, jnp.int32) for _ in range(blocks)]
    for v in reversed(range(blocks * per_block)):
        col = cols[8 * v : 8 * v + 8, :]
        for b in range(v // per_block, blocks):
            first[b] = jnp.where(col == rows[b], v, first[b])
    sublane = lax.broadcasted_iota(jnp.int32, (8, LANES), 0)
    lane = lax.broadcasted_iota(jnp.int32, (1, LANES), 1)
    leads = [
        jnp.min(first[b] * 8 + sublane, axis=0, keepdims=True) == lane + b * LANES for b in range(blocks)
    ]

    device = lax.broadcasted_iota(jnp.int32, (devices, LANES), 0)
    owned = [device == owner[b : b + 1, :] for b in range(blocks)]
    hot = [owned[b] & leads[b] for b in range(blocks)]
    hot16 = jnp.concatenate([h.astype(jnp.float32) for h in hot], axis=0).astype(jnp.bfloat16)
    i0 = lax.broadcasted_iota(jnp.int32, (LANES, 2 * LANES), 0)
    i1 = lax.broadcasted_iota(jnp.int32, (LANES, 2 * LANES), 1)
    ahead = ((i0 < i1)).astype(jnp.float32).astype(jnp.bfloat16)
    counted = jnp.dot(hot16, ahead, preferred_element_type=jnp.float32)
    counts = jnp.zeros((devices, LANES), jnp.float32)
    header_high = jnp.zeros((devices, LANES), jnp.float32)
    header_low = jnp.zeros((devices, LANES), jnp.float32)
    slot_high, slot_low = split(slot, LANES)
    lanes = lax.broadcasted_iota(jnp.int32, (LANES, LANES), 1)
    for b in range(blocks):
        here = counted[b * devices : (b + 1) * devices]
        rank = jnp.sum(jnp.where(owned[b], here[:, :LANES] + counts, 0.0), axis=0, keepdims=True)
        counts = counts + here[:, LANES:]
        rank_col = column(rank.astype(jnp.int32))
        marks[b * LANES : (b + 1) * LANES, :] = rank_col
        place = (rank_col == lanes).astype(jnp.float32).astype(jnp.bfloat16)
        both = jnp.concatenate(
            [
                jnp.where(hot[b], slot_high[b : b + 1, :].astype(jnp.float32), 0.0),
                jnp.where(hot[b], slot_low[b : b + 1, :].astype(jnp.float32), 0.0),
            ],
            axis=0,
        ).astype(jnp.bfloat16)
        parts = jnp.dot(both, place, preferred_element_type=jnp.float32)
        header_high = header_high + parts[:devices]
        header_low = header_low + parts[devices:]

    ranks = [jnp.full((8, LANES), drop, jnp.int32) for _ in range(blocks)]
    for v in reversed(range(blocks * per_block)):
        col = cols[8 * v : 8 * v + 8, :]
        mark = marks[8 * v : 8 * v + 8, :]
        for b in range(v // per_block, blocks):
            ranks[b] = jnp.where(col == rows[b], mark, ranks[b])
    rank = jnp.concatenate([jnp.min(r, axis=0, keepdims=True) for r in ranks], axis=0)
    target_vmem[...] = jnp.where(rank < slots, owner * width + rank, drop)
    send_target = pltpu.make_async_copy(target_vmem, target, sems.at[1])
    send_target.start()
    info_ref[0:blocks, :] = rank
    info_ref[blocks : 2 * blocks, :] = position

    for s in range(STREAMS):
        sums[s][...] = jnp.zeros_like(sums[s])
    over = jnp.max(counts) > slots
    header = jnp.where(
        lane.astype(jnp.float32) < jnp.minimum(counts, slots), header_high * LANES + header_low, float(rows_dev)
    )
    header = jnp.where(lane == LANES - 1, jnp.minimum(counts, slots), header)
    header = jnp.where(lane == LANES - 2, jnp.where(over, 1.0, 0.0), header)
    send_target.wait()
    fetch.wait()

    @pl.loop(0, blocks)
    def _(b):
        @pl.loop(0, LANES // UNROLL)
        def _(q):
            c0 = q * UNROLL
            at = [target[b, c0 + u] for u in range(UNROLL)]
            for g in range(0, UNROLL, STREAMS):
                old = [sums[s][pl.ds(at[g + s], 1), :] for s in range(STREAMS)]
                new = [
                    old[s] + grad_ref[pl.ds(b * LANES + c0 + g + s, 1), :] for s in range(STREAMS)
                ]
                for s in range(STREAMS):
                    sums[s][pl.ds(at[g + s], 1), :] = new[s]

    total = sums[0][0:drop, :]
    for s in range(1, STREAMS):
        total = total + sums[s][0:drop, :]
    send_ref[...] = total
    send_ref[pl.ds(slots, devices, stride=width), :] = header


def update_kernel(
    devices, got_ref, more_head_ref, more_hbm, accum_ref, table_hbm, table_out, accum_out,
    sums, table, more, head_vmem, head, sems_in, sems_out, sem,
):
    width = got_ref.shape[0] // devices
    slots = width - 1
    more_width = more_hbm.shape[0] // devices
    rows_dev = table.shape[0]
    chunk = rows_dev // CHUNKS
    unroll = UNROLL if width % UNROLL == 0 else 8
    head_vmem[0:devices, :] = got_ref[pl.ds(slots, devices, stride=width), :].astype(jnp.int32)
    head_vmem[devices : 2 * devices, :] = more_head_ref[...]
    load_head = pltpu.make_async_copy(head_vmem, head, sem)
    load_head.start()
    loads = [
        pltpu.make_async_copy(
            table_hbm.at[pl.ds(c * chunk, chunk), :], table.at[pl.ds(c * chunk, chunk), :], sems_in.at[c]
        )
        for c in range(CHUNKS)
    ]
    for load in loads:
        load.start()
    sums[...] = jnp.zeros_like(sums)
    load_head.wait()

    def add_rows(source_head, rows_ref, base, count):
        @pl.loop(0, lax.div(count + unroll - 1, unroll))
        def _(q):
            r0 = q * unroll
            at = [head[source_head, r0 + u] for u in range(unroll)]
            old = [sums[pl.ds(a, 1), :] for a in at]
            new = [old[u] + rows_ref[pl.ds(base + r0 + u, 1), :] for u in range(unroll)]
            for u in range(unroll):
                sums[pl.ds(at[u], 1), :] = new[u]

    @pl.loop(0, devices)
    def _(d):
        add_rows(d, got_ref, d * width, head[d, LANES - 1])

    @pl.loop(0, devices)
    def _(d):
        @pl.when(head[devices + d, LANES - 1] > 0)
        def _():
            copy = pltpu.make_async_copy(
                more_hbm.at[pl.ds(d * more_width, more_width), :], more.at[pl.ds(0, more_width), :], sem
            )
            copy.start()
            copy.wait()
            add_rows(devices + d, more, 0, head[devices + d, LANES - 1])

    groups = chunk // LANES
    stores = []
    for c in range(CHUNKS):
        loads[c].wait()

        @pl.loop(0, groups)
        def _(i):
            k = c * groups + i
            here = pl.ds(pl.multiple_of(k * LANES, LANES), LANES)
            grad = sums[here, :]
            mean = jnp.sum(jnp.transpose(grad * grad), axis=0, keepdims=True) * (1.0 / LANES)
            new_accum = accum_ref[pl.ds(k, 1), :] + mean
            accum_out[pl.ds(k, 1), :] = new_accum
            scale = learning_rate / (jnp.sqrt(new_accum) + epsilon)
            table[here, :] = table[here, :] - jnp.transpose(jnp.broadcast_to(scale, (LANES, LANES))) * grad

        store = pltpu.make_async_copy(
            table.at[pl.ds(c * chunk, chunk), :], table_out.at[pl.ds(c * chunk, chunk), :], sems_out.at[c]
        )
        store.start()
        stores.append(store)
    for store in stores:
        store.wait()


def on_device(row_ids, block_map, grad_tiles, table, accum):
    axes = ("gx", "gy")
    devices = lax.axis_size("gx") * lax.axis_size("gy")
    rows_dev, features = table.shape
    look_count = row_ids.shape[0]
    capacity = 2 * look_count // devices
    width = -(-capacity * 13 // 16 // 8) * 8
    slots = width - 1
    more_slots = -(-(capacity - slots) // UNROLL) * UNROLL
    blocks = look_count // LANES
    vmem = pl.BlockSpec(memory_space=pltpu.VMEM)
    hbm = pl.BlockSpec(memory_space=pl.ANY)

    send, info = pl.pallas_call(
        functools.partial(bin_kernel, devices, rows_dev),
        out_shape=(
            jax.ShapeDtypeStruct((devices * width, features), jnp.float32),
            jax.ShapeDtypeStruct((2 * blocks, LANES), jnp.int32),
        ),
        in_specs=[vmem, vmem, hbm],
        out_specs=(vmem, vmem),
        scratch_shapes=[
            pltpu.VMEM((look_count, features), jnp.float32),
            pltpu.VMEM((look_count, LANES), jnp.int32),
            pltpu.VMEM((look_count, LANES), jnp.int32),
            pltpu.VMEM((blocks, LANES), jnp.int32),
            pltpu.SMEM((blocks, LANES), jnp.int32),
            [pltpu.VMEM((devices * width + 8, features), jnp.float32)] * STREAMS,
            pltpu.SemaphoreType.DMA((2,)),
        ],
        compiler_params=pltpu.CompilerParams(vmem_limit_bytes=24 << 20),
        name="bin_rows",
    )(row_ids.reshape(blocks, LANES), block_map.reshape(-1, LANES), grad_tiles)

    got = lax.all_to_all(send, axes, split_axis=0, concat_axis=0, tiled=True)

    def second_round(_):
        rank, position = info[:blocks].reshape(-1), info[blocks:].reshape(-1)
        owner, slot = position // rows_dev, position % rows_dev
        limit = devices * more_slots
        at = jnp.where(rank >= slots, owner * more_slots + rank - slots, limit)
        rows = jnp.zeros((limit, features), jnp.float32).at[at].add(grad_tiles, mode="drop")
        places = jnp.full((limit,), rows_dev, jnp.int32).at[at].set(slot, mode="drop")
        rows = lax.all_to_all(rows, axes, split_axis=0, concat_axis=0, tiled=True)
        places = lax.all_to_all(places, axes, split_axis=0, concat_axis=0, tiled=True)
        places = places.reshape(devices, more_slots)
        count = jnp.sum((places < rows_dev).astype(jnp.int32), axis=1, keepdims=True)
        places = jnp.pad(places, ((0, 0), (0, LANES - 1 - more_slots)), constant_values=rows_dev)
        return rows, jnp.concatenate([places, count], axis=1)

    def one_round(_):
        return (
            jnp.zeros((devices * more_slots, features), jnp.float32),
            jnp.zeros((devices, LANES), jnp.int32),
        )

    over = jnp.max(got.reshape(devices, width, features)[:, slots, LANES - 2]) > 0.5
    more, more_head = lax.cond(over, second_round, one_round, None)

    new_table, new_accum = pl.pallas_call(
        functools.partial(update_kernel, devices),
        out_shape=(
            jax.ShapeDtypeStruct(table.shape, jnp.float32),
            jax.ShapeDtypeStruct((rows_dev // LANES, LANES), jnp.float32),
        ),
        in_specs=[vmem, vmem, hbm, vmem, hbm],
        out_specs=(hbm, vmem),
        scratch_shapes=[
            pltpu.VMEM((rows_dev + 8, features), jnp.float32),
            pltpu.VMEM((rows_dev, features), jnp.float32),
            pltpu.VMEM((more_slots + UNROLL, features), jnp.float32),
            pltpu.VMEM((2 * devices, LANES), jnp.int32),
            pltpu.SMEM((2 * devices, LANES), jnp.int32),
            pltpu.SemaphoreType.DMA((CHUNKS,)),
            pltpu.SemaphoreType.DMA((CHUNKS,)),
            pltpu.SemaphoreType.DMA(()),
        ],
        compiler_params=pltpu.CompilerParams(vmem_limit_bytes=24 << 20),
        name="apply_step",
    )(got, more_head, more, accum.reshape(-1, LANES), table)
    return new_table, new_accum.reshape(-1)


def solution(mesh):
    in_specs = (P(("gx", "gy")), P(), P(("gx", "gy"), None), P(("gx", "gy"), None), P(("gx", "gy")))
    out_specs = (P(("gx", "gy"), None), P(("gx", "gy")))
    return jax.shard_map(
        on_device, mesh=mesh, in_specs=in_specs, out_specs=out_specs, check_vma=False
    )
```

```python
import functools

import jax
import jax.numpy as jnp
from jax import lax
from jax.experimental import pallas as pl
from jax.experimental.pallas import tpu as pltpu
from jax.sharding import PartitionSpec as P

BLOCK = 128
LANES = 128
STREAMS = 4
UNROLL = 16
CHUNKS = 8

learning_rate = 0.25
epsilon = 1e-08


def split(x, n):
    if n & (n - 1) == 0:
        return lax.shift_right_logical(x, n.bit_length() - 1), x & (n - 1)
    return lax.div(x, n), lax.rem(x, n)


def bin_kernel(
    devices, rows_dev, ids_hbm, map_hbm, grad_hbm, send_ref, info_ref, ids_ref, map_ref, grad_ref, cols, marks, target_vmem, target, sums, sems
):
    blocks = ids_ref.shape[0]
    width = send_ref.shape[0] // devices
    slots = width - 1
    drop = devices * width
    fetch = pltpu.make_async_copy(grad_hbm, grad_ref, sems.at[0])
    fetch_ids = pltpu.make_async_copy(ids_hbm, ids_ref, sems.at[1])
    fetch_map = pltpu.make_async_copy(map_hbm, map_ref, sems.at[2])
    fetch_ids.start()
    fetch_map.start()
    fetch.start()
    fetch_ids.wait()
    fetch_map.wait()

    block, within = split(ids_ref[...], BLOCK)
    high, low = split(block, LANES)
    mapped = jnp.zeros_like(block)
    for h in range(map_ref.shape[0]):
        row = jnp.broadcast_to(map_ref[h : h + 1, :], low.shape)
        mapped = jnp.where(high == h, jnp.take_along_axis(row, low, axis=1), mapped)
    position = mapped * BLOCK + within
    owner, slot = split(position, rows_dev)

    def column(row):
        return jnp.transpose(jnp.broadcast_to(row, (LANES, LANES)))

    for b in range(blocks):
        cols[b * LANES : (b + 1) * LANES, :] = column(position[b : b + 1, :])
    rows = [jnp.broadcast_to(position[b : b + 1, :], (8, LANES)) for b in range(blocks)]
    per_block = LANES // 8
    none = blocks * per_block
    first = [jnp.full((8, LANES), none, jnp.int32) for _ in range(blocks)]
    for v in reversed(range(blocks * per_block)):
        col = cols[8 * v : 8 * v + 8, :]
        for b in range(v // per_block, blocks):
            first[b] = jnp.where(col == rows[b], v, first[b])
    sublane = lax.broadcasted_iota(jnp.int32, (8, LANES), 0)
    lane = lax.broadcasted_iota(jnp.int32, (1, LANES), 1)
    leads = [
        jnp.min(first[b] * 8 + sublane, axis=0, keepdims=True) == lane + b * LANES for b in range(blocks)
    ]

    device = lax.broadcasted_iota(jnp.int32, (devices, LANES), 0)
    owned = [device == owner[b : b + 1, :] for b in range(blocks)]
    hot = [owned[b] & leads[b] for b in range(blocks)]
    hot16 = jnp.concatenate([h.astype(jnp.float32) for h in hot], axis=0).astype(jnp.bfloat16)
    i0 = lax.broadcasted_iota(jnp.int32, (LANES, 2 * LANES), 0)
    i1 = lax.broadcasted_iota(jnp.int32, (LANES, 2 * LANES), 1)
    ahead = ((i0 < i1)).astype(jnp.float32).astype(jnp.bfloat16)
    counted = jnp.dot(hot16, ahead, preferred_element_type=jnp.float32)
    counts = jnp.zeros((devices, LANES), jnp.float32)
    header_high = jnp.zeros((devices, LANES), jnp.float32)
    header_low = jnp.zeros((devices, LANES), jnp.float32)
    slot_high, slot_low = split(slot, LANES)
    lanes = lax.broadcasted_iota(jnp.int32, (LANES, LANES), 1)
    for b in range(blocks):
        here = counted[b * devices : (b + 1) * devices]
        rank = jnp.sum(jnp.where(owned[b], here[:, :LANES] + counts, 0.0), axis=0, keepdims=True)
        counts = counts + here[:, LANES:]
        rank_col = column(rank.astype(jnp.int32))
        marks[b * LANES : (b + 1) * LANES, :] = rank_col
        place = (rank_col == lanes).astype(jnp.float32).astype(jnp.bfloat16)
        both = jnp.concatenate(
            [
                jnp.where(hot[b], slot_high[b : b + 1, :].astype(jnp.float32), 0.0),
                jnp.where(hot[b], slot_low[b : b + 1, :].astype(jnp.float32), 0.0),
            ],
            axis=0,
        ).astype(jnp.bfloat16)
        parts = jnp.dot(both, place, preferred_element_type=jnp.float32)
        header_high = header_high + parts[:devices]
        header_low = header_low + parts[devices:]

    ranks = [jnp.full((8, LANES), drop, jnp.int32) for _ in range(blocks)]
    for v in reversed(range(blocks * per_block)):
        col = cols[8 * v : 8 * v + 8, :]
        mark = marks[8 * v : 8 * v + 8, :]
        for b in range(v // per_block, blocks):
            ranks[b] = jnp.where(col == rows[b], mark, ranks[b])
    rank = jnp.concatenate([jnp.min(r, axis=0, keepdims=True) for r in ranks], axis=0)
    target_vmem[...] = jnp.where(rank < slots, owner * width + rank, drop)
    send_target = pltpu.make_async_copy(target_vmem, target, sems.at[3])
    send_target.start()
    info_ref[0:blocks, :] = rank
    info_ref[blocks : 2 * blocks, :] = position

    for s in range(STREAMS):
        sums[s][...] = jnp.zeros_like(sums[s])
    over = jnp.max(counts) > slots
    header = jnp.where(
        lane.astype(jnp.float32) < jnp.minimum(counts, slots), header_high * LANES + header_low, float(rows_dev)
    )
    header = jnp.where(lane == LANES - 1, jnp.minimum(counts, slots), header)
    header = jnp.where(lane == LANES - 2, jnp.where(over, 1.0, 0.0), header)
    send_target.wait()
    fetch.wait()

    @pl.loop(0, blocks)
    def _(b):
        for c0 in range(0, LANES, STREAMS):
            at = [target[b, c0 + s] for s in range(STREAMS)]
            old = [sums[s][pl.ds(at[s], 1), :] for s in range(STREAMS)]
            new = [old[s] + grad_ref[pl.ds(b * LANES + c0 + s, 1), :] for s in range(STREAMS)]
            for s in range(STREAMS):
                sums[s][pl.ds(at[s], 1), :] = new[s]

    total = sums[0][0:drop, :]
    for s in range(1, STREAMS):
        total = total + sums[s][0:drop, :]
    send_ref[...] = total
    send_ref[pl.ds(slots, devices, stride=width), :] = header


def update_kernel(
    devices, rounds, *refs
):
    if rounds == 2:
        more_head_ref, more_ref, *refs = refs
    got_ref, accum_ref, table_hbm, table_out, accum_out, sums, table, head_vmem, head, sems_in, sems_out, sem = refs
    width = got_ref.shape[0] // devices
    slots = width - 1
    rows_dev = table.shape[0]
    chunk = rows_dev // CHUNKS
    unroll = UNROLL if width % UNROLL == 0 else 8
    head_vmem[0:devices, :] = got_ref[pl.ds(slots, devices, stride=width), :].astype(jnp.int32)
    if rounds == 2:
        head_vmem[devices : 2 * devices, :] = more_head_ref[...]
    load_head = pltpu.make_async_copy(head_vmem, head, sem)
    load_head.start()
    loads = [
        pltpu.make_async_copy(
            table_hbm.at[pl.ds(c * chunk, chunk), :], table.at[pl.ds(c * chunk, chunk), :], sems_in.at[c]
        )
        for c in range(CHUNKS)
    ]
    for load in loads:
        load.start()
    sums[...] = jnp.zeros_like(sums)
    load_head.wait()

    def add_rows(source_head, rows_ref, base, limit):
        count = head[source_head, LANES - 1]
        for r0 in range(0, limit, unroll):

            @pl.when(count > r0)
            def _():
                at = [head[source_head, r0 + u] for u in range(unroll)]
                old = [sums[pl.ds(a, 1), :] for a in at]
                new = [old[u] + rows_ref[pl.ds(base + r0 + u, 1), :] for u in range(unroll)]
                for u in range(unroll):
                    sums[pl.ds(at[u], 1), :] = new[u]

    @pl.loop(0, devices)
    def _(d):
        add_rows(d, got_ref, d * width, slots)

    if rounds == 2:
        more_width = more_ref.shape[0] // devices

        @pl.loop(0, devices)
        def _(d):
            add_rows(devices + d, more_ref, d * more_width, more_width)

    groups = chunk // LANES
    stores = []
    for c in range(CHUNKS):
        heres = [pl.ds((c * groups + i) * LANES, LANES) for i in range(groups)]
        these = pl.ds(c * groups, groups)
        squares = [jnp.transpose(jnp.square(sums[here, :])) for here in heres]
        totals = jnp.concatenate([jnp.sum(x, axis=0, keepdims=True) for x in squares], axis=0)
        new_accum = accum_ref[these, :] + totals * (1.0 / LANES)
        accum_out[these, :] = new_accum
        scale = learning_rate / (jnp.sqrt(new_accum) + epsilon)
        loads[c].wait()
        for i, here in enumerate(heres):
            factor = jnp.transpose(jnp.broadcast_to(scale[i : i + 1, :], (LANES, LANES)))
            table[here, :] = table[here, :] - factor * sums[here, :]

        store = pltpu.make_async_copy(
            table.at[pl.ds(c * chunk, chunk), :], table_out.at[pl.ds(c * chunk, chunk), :], sems_out.at[c]
        )
        store.start()
        stores.append(store)
    for store in stores:
        store.wait()


def on_device(row_ids, block_map, grad_tiles, table, accum):
    axes = ("gx", "gy")
    devices = lax.axis_size("gx") * lax.axis_size("gy")
    rows_dev, features = table.shape
    look_count = row_ids.shape[0]
    capacity = 2 * look_count // devices
    width = -(-capacity * 13 // 16 // 8) * 8
    slots = width - 1
    more_slots = -(-(capacity - slots) // UNROLL) * UNROLL
    blocks = look_count // LANES
    vmem = pl.BlockSpec(memory_space=pltpu.VMEM)
    hbm = pl.BlockSpec(memory_space=pltpu.MemorySpace.HBM)

    send, info = pl.pallas_call(
        functools.partial(bin_kernel, devices, rows_dev),
        out_shape=(
            jax.ShapeDtypeStruct((devices * width, features), jnp.float32),
            jax.ShapeDtypeStruct((2 * blocks, LANES), jnp.int32),
        ),
        in_specs=[hbm, hbm, hbm],
        out_specs=(vmem, vmem),
        scratch_shapes=[
            pltpu.VMEM((blocks, LANES), jnp.int32),
            pltpu.VMEM((block_map.shape[0] // LANES, LANES), jnp.int32),
            pltpu.VMEM((look_count, features), jnp.float32),
            pltpu.VMEM((look_count, LANES), jnp.int32),
            pltpu.VMEM((look_count, LANES), jnp.int32),
            pltpu.VMEM((blocks, LANES), jnp.int32),
            pltpu.SMEM((blocks, LANES), jnp.int32),
            [pltpu.VMEM((devices * width + 8, features), jnp.float32)] * STREAMS,
            pltpu.SemaphoreType.DMA((4,)),
        ],
        compiler_params=pltpu.CompilerParams(vmem_limit_bytes=24 << 20),
        name="bin_rows",
    )(row_ids.reshape(blocks, LANES), block_map.reshape(-1, LANES), grad_tiles)

    got = lax.all_to_all(send, axes, split_axis=0, concat_axis=0, tiled=True)

    def apply_step(rounds, *args):
        new_table, new_accum = pl.pallas_call(
            functools.partial(update_kernel, devices, rounds),
            out_shape=(
                jax.ShapeDtypeStruct(table.shape, jnp.float32),
                jax.ShapeDtypeStruct((rows_dev // LANES, LANES), jnp.float32),
            ),
            in_specs=[vmem] * (2 * rounds) + [hbm],
            out_specs=(hbm, vmem),
            scratch_shapes=[
                pltpu.VMEM((rows_dev + 8, features), jnp.float32),
                pltpu.VMEM((rows_dev, features), jnp.float32),
                pltpu.VMEM((rounds * devices, LANES), jnp.int32),
                pltpu.SMEM((rounds * devices, LANES), jnp.int32),
                pltpu.SemaphoreType.DMA((CHUNKS,)),
                pltpu.SemaphoreType.DMA((CHUNKS,)),
                pltpu.SemaphoreType.DMA(()),
            ],
            compiler_params=pltpu.CompilerParams(vmem_limit_bytes=24 << 20),
            name=f"apply_step_{rounds}",
        )(*args, got, accum.reshape(-1, LANES), table)
        return new_table, new_accum.reshape(-1)

    def two_rounds():
        rank, position = info[:blocks].reshape(-1), info[blocks:].reshape(-1)
        owner, slot = position // rows_dev, position % rows_dev
        limit = devices * more_slots
        at = jnp.where(rank >= slots, owner * more_slots + rank - slots, limit)
        rows = jnp.zeros((limit, features), jnp.float32).at[at].add(grad_tiles, mode="drop")
        places = jnp.full((limit,), rows_dev, jnp.int32).at[at].set(slot, mode="drop")
        rows = lax.all_to_all(rows, axes, split_axis=0, concat_axis=0, tiled=True)
        places = lax.all_to_all(places, axes, split_axis=0, concat_axis=0, tiled=True)
        places = places.reshape(devices, more_slots)
        count = jnp.sum((places < rows_dev).astype(jnp.int32), axis=1, keepdims=True)
        places = jnp.pad(places, ((0, 0), (0, LANES - 1 - more_slots)), constant_values=rows_dev)
        return apply_step(2, jnp.concatenate([places, count], axis=1), rows)

    over = jnp.max(got.reshape(devices, width, features)[:, slots, LANES - 2]) > 0.5
    return lax.cond(over, two_rounds, lambda: apply_step(1))


def solution(mesh):
    in_specs = (P(("gx", "gy")), P(), P(("gx", "gy"), None), P(("gx", "gy"), None), P(("gx", "gy")))
    out_specs = (P(("gx", "gy"), None), P(("gx", "gy")))
    return jax.shard_map(
        on_device, mesh=mesh, in_specs=in_specs, out_specs=out_specs, check_vma=False
    )
```

```python
import functools

import jax
import jax.numpy as jnp
from jax import lax
from jax.experimental import pallas as pl
from jax.experimental.pallas import tpu as pltpu
from jax.sharding import PartitionSpec as P

BLOCK = 128
LANES = 128
STREAMS = 4
UNROLL = 16
CHUNKS = 8

learning_rate = 0.25
epsilon = 1e-08


def split(x, n):
    if n & (n - 1) == 0:
        return lax.shift_right_logical(x, n.bit_length() - 1), x & (n - 1)
    return lax.div(x, n), lax.rem(x, n)


def bin_kernel(
    devices, group, spare, rows_dev, ids_hbm, map_hbm, grad_hbm, send_ref, info_ref, ids_ref, map_ref, grad_ref, cols, marks, target_vmem, target, sums, sems
):
    blocks = ids_ref.shape[0]
    width = send_ref.shape[0] // devices
    slots = width - 1
    drop = devices * width
    fetch = pltpu.make_async_copy(grad_hbm, grad_ref, sems.at[0])
    fetch_ids = pltpu.make_async_copy(ids_hbm, ids_ref, sems.at[1])
    fetch_map = pltpu.make_async_copy(map_hbm, map_ref, sems.at[2])
    fetch_ids.start()
    fetch_map.start()
    fetch.start()
    fetch_ids.wait()
    fetch_map.wait()

    block, within = split(ids_ref[...], BLOCK)
    high, low = split(block, LANES)
    mapped = jnp.zeros_like(block)
    for h in range(map_ref.shape[0]):
        row = jnp.broadcast_to(map_ref[h : h + 1, :], low.shape)
        mapped = jnp.where(high == h, jnp.take_along_axis(row, low, axis=1), mapped)
    position = mapped * BLOCK + within
    owner, slot = split(position, rows_dev)

    def column(row):
        return jnp.transpose(jnp.broadcast_to(row, (LANES, LANES)))

    for b in range(blocks):
        cols[b * LANES : (b + 1) * LANES, :] = column(position[b : b + 1, :])
    rows = [jnp.broadcast_to(position[b : b + 1, :], (8, LANES)) for b in range(blocks)]
    per_block = LANES // 8
    none = blocks * per_block
    first = [jnp.full((8, LANES), none, jnp.int32) for _ in range(blocks)]
    for v in reversed(range(blocks * per_block)):
        col = cols[8 * v : 8 * v + 8, :]
        for b in range(v // per_block, blocks):
            first[b] = jnp.where(col == rows[b], v, first[b])
    sublane = lax.broadcasted_iota(jnp.int32, (8, LANES), 0)
    lane = lax.broadcasted_iota(jnp.int32, (1, LANES), 1)
    leads = [
        jnp.min(first[b] * 8 + sublane, axis=0, keepdims=True) == lane + b * LANES for b in range(blocks)
    ]

    device = lax.broadcasted_iota(jnp.int32, (devices, LANES), 0)
    owned = [device == owner[b : b + 1, :] for b in range(blocks)]
    hot = [owned[b] & leads[b] for b in range(blocks)]
    hot16 = jnp.concatenate([h.astype(jnp.float32) for h in hot], axis=0).astype(jnp.bfloat16)
    i0 = lax.broadcasted_iota(jnp.int32, (LANES, 2 * LANES), 0)
    i1 = lax.broadcasted_iota(jnp.int32, (LANES, 2 * LANES), 1)
    ahead = ((i0 < i1)).astype(jnp.float32).astype(jnp.bfloat16)
    counted = jnp.dot(hot16, ahead, preferred_element_type=jnp.float32)
    counts = jnp.zeros((devices, LANES), jnp.float32)
    ranks = []
    for b in range(blocks):
        here = counted[b * devices : (b + 1) * devices]
        ranks.append(jnp.sum(jnp.where(owned[b], here[:, :LANES] + counts, 0.0), axis=0, keepdims=True))
        counts = counts + here[:, LANES:]

    def partner(x):
        parts = [x[i : i + group] for i in range(0, devices, group)]
        return jnp.concatenate([parts[i ^ 1] for i in range(len(parts))], axis=0)

    kept = jnp.minimum(counts, slots)
    extra = counts - kept
    fits = (extra <= spare) & (partner(kept) + extra <= slots)
    shift = jnp.where(fits, slots - counts, -2.0 * LANES)
    guests = partner(jnp.where(fits, extra, 0.0))

    header_high = jnp.zeros((devices, LANES), jnp.float32)
    header_low = jnp.zeros((devices, LANES), jnp.float32)
    slot_high, slot_low = split(slot, LANES)
    lanes = lax.broadcasted_iota(jnp.int32, (LANES, LANES), 1)
    nowhere = devices * LANES
    for b in range(blocks):
        moved = ranks[b] + jnp.sum(jnp.where(owned[b], shift, 0.0), axis=0, keepdims=True)
        at_home = ranks[b] < slots
        mine = owner[b : b + 1, :]
        across, _ = split(mine, group)
        other = mine + jnp.where((across & 1) == 0, group, -group)
        bin_of = jnp.where(at_home, mine, jnp.where(moved >= 0.0, other, devices))
        row_of = jnp.where(at_home, ranks[b], jnp.where(moved >= 0.0, moved, 0.0)).astype(jnp.int32)
        bin_of = jnp.where(leads[b], bin_of, devices)
        mark_col = column(jnp.where(bin_of < devices, bin_of * LANES + row_of, nowhere))
        marks[b * LANES : (b + 1) * LANES, :] = mark_col
        place = ((mark_col & (LANES - 1)) == lanes).astype(jnp.float32).astype(jnp.bfloat16)
        sent = device == bin_of
        both = jnp.concatenate(
            [
                jnp.where(sent, slot_high[b : b + 1, :].astype(jnp.float32), 0.0),
                jnp.where(sent, slot_low[b : b + 1, :].astype(jnp.float32), 0.0),
            ],
            axis=0,
        ).astype(jnp.bfloat16)
        parts = jnp.dot(both, place, preferred_element_type=jnp.float32)
        header_high = header_high + parts[:devices]
        header_low = header_low + parts[devices:]

    best = [jnp.full((8, LANES), nowhere, jnp.int32) for _ in range(blocks)]
    for v in reversed(range(blocks * per_block)):
        col = cols[8 * v : 8 * v + 8, :]
        mark = marks[8 * v : 8 * v + 8, :]
        for b in range(v // per_block, blocks):
            best[b] = jnp.where(col == rows[b], jnp.minimum(mark, best[b]), best[b])
    mark = jnp.concatenate([jnp.min(x, axis=0, keepdims=True) for x in best], axis=0)
    target_vmem[...] = jnp.where(
        mark < nowhere, lax.shift_right_logical(mark, 7) * width + (mark & (LANES - 1)), drop
    )
    send_target = pltpu.make_async_copy(target_vmem, target, sems.at[3])
    send_target.start()
    info_ref[0:blocks, :] = mark
    info_ref[blocks : 2 * blocks, :] = position

    for s in range(STREAMS):
        sums[s][...] = jnp.zeros_like(sums[s])
    over = jnp.max(jnp.where(fits, 0.0, 1.0))
    header = header_high * LANES + header_low
    header = jnp.where(lane == LANES - 1, kept, header)
    header = jnp.where(lane == LANES - 2, over, header)
    header = jnp.where(lane == LANES - 3, guests, header)
    send_target.wait()
    fetch.wait()

    @pl.loop(0, blocks)
    def _(b):
        for c0 in range(0, LANES, STREAMS):
            at = [target[b, c0 + s] for s in range(STREAMS)]
            old = [sums[s][pl.ds(at[s], 1), :] for s in range(STREAMS)]
            new = [old[s] + grad_ref[pl.ds(b * LANES + c0 + s, 1), :] for s in range(STREAMS)]
            for s in range(STREAMS):
                sums[s][pl.ds(at[s], 1), :] = new[s]

    total = sums[0][0:drop, :]
    for s in range(1, STREAMS):
        total = total + sums[s][0:drop, :]
    send_ref[...] = total
    send_ref[pl.ds(slots, devices, stride=width), :] = header


def update_kernel(
    devices, rounds, *refs
):
    if rounds == 2:
        more_head_ref, more_ref, *refs = refs
    got_ref, guest_ref, accum_ref, table_hbm, table_out, accum_out, sums, table, head_vmem, head, sems_in, sems_out, sem = refs
    width = got_ref.shape[0] // devices
    slots = width - 1
    rows_dev = table.shape[0]
    chunk = rows_dev // CHUNKS
    unroll = UNROLL if width % UNROLL == 0 else 8
    guest_width = guest_ref.shape[0] // devices
    lane = lax.broadcasted_iota(jnp.int32, (devices, LANES), 1)
    last = LANES - 1
    own = got_ref[pl.ds(slots, devices, stride=width), :].astype(jnp.int32)
    head_vmem[0:devices, :] = jnp.where((lane < own[:, last:]) | (lane == last), own, rows_dev)
    guest = guest_ref[pl.ds(guest_width - 1, devices, stride=guest_width), :].astype(jnp.int32)
    guests = guest[:, last - 2 : last - 1]
    head_vmem[devices : 2 * devices, :] = jnp.where(
        lane == last, guests, jnp.where((lane >= slots - guests) & (lane < slots), guest, rows_dev)
    )
    if rounds == 2:
        head_vmem[2 * devices : 3 * devices, :] = more_head_ref[...]
    load_head = pltpu.make_async_copy(head_vmem, head, sem)
    load_head.start()
    loads = [
        pltpu.make_async_copy(
            table_hbm.at[pl.ds(c * chunk, chunk), :], table.at[pl.ds(c * chunk, chunk), :], sems_in.at[c]
        )
        for c in range(CHUNKS)
    ]
    for load in loads:
        load.start()
    sums[...] = jnp.zeros_like(sums)
    load_head.wait()

    def add_group(source, c0, rows_ref, base, size):
        at = [head[source, c0 + u] for u in range(size)]
        old = [sums[pl.ds(a, 1), :] for a in at]
        new = [old[u] + rows_ref[pl.ds(base + u, 1), :] for u in range(size)]
        for u in range(size):
            sums[pl.ds(at[u], 1), :] = new[u]

    def add_rows(source, rows_ref, base, limit):
        count = head[source, LANES - 1]
        for r0 in range(0, limit, unroll):

            @pl.when(count > r0)
            def _():
                add_group(source, r0, rows_ref, base + r0, unroll)

    @pl.loop(0, devices)
    def _(d):
        add_rows(d, got_ref, d * width, slots)
        guests = head[devices + d, LANES - 1]
        for r0 in range(guest_width - 8, -1, -8):

            @pl.when(guests > max(guest_width - 9 - r0, 0))
            def _():
                add_group(devices + d, width - guest_width + r0, guest_ref, d * guest_width + r0, 8)


    if rounds == 2:
        more_width = more_ref.shape[0] // devices

        @pl.loop(0, devices)
        def _(d):
            add_rows(2 * devices + d, more_ref, d * more_width, more_width)

    groups = chunk // LANES
    stores = []
    for c in range(CHUNKS):
        heres = [pl.ds((c * groups + i) * LANES, LANES) for i in range(groups)]
        these = pl.ds(c * groups, groups)
        squares = [jnp.transpose(jnp.square(sums[here, :])) for here in heres]
        totals = jnp.concatenate([jnp.sum(x, axis=0, keepdims=True) for x in squares], axis=0)
        new_accum = accum_ref[these, :] + totals * (1.0 / LANES)
        accum_out[these, :] = new_accum
        scale = learning_rate / (jnp.sqrt(new_accum) + epsilon)
        loads[c].wait()
        for i, here in enumerate(heres):
            factor = jnp.transpose(jnp.broadcast_to(scale[i : i + 1, :], (LANES, LANES)))
            table[here, :] = table[here, :] - factor * sums[here, :]

        store = pltpu.make_async_copy(
            table.at[pl.ds(c * chunk, chunk), :], table_out.at[pl.ds(c * chunk, chunk), :], sems_out.at[c]
        )
        store.start()
        stores.append(store)
    for store in stores:
        store.wait()


def on_device(row_ids, block_map, grad_tiles, table, accum):
    axes = ("gx", "gy")
    devices = lax.axis_size("gx") * lax.axis_size("gy")
    rows_dev, features = table.shape
    look_count = row_ids.shape[0]
    capacity = 2 * look_count // devices
    width = -(-capacity * 5 // 8 // 8) * 8
    guest_width = -(-width * 3 // 10 // 8) * 8
    slots = width - 1
    more_slots = -(-(capacity - slots) // UNROLL) * UNROLL
    blocks = look_count // LANES
    vmem = pl.BlockSpec(memory_space=pltpu.VMEM)
    hbm = pl.BlockSpec(memory_space=pltpu.MemorySpace.HBM)

    send, info = pl.pallas_call(
        functools.partial(bin_kernel, devices, lax.axis_size("gy"), guest_width - 1, rows_dev),
        out_shape=(
            jax.ShapeDtypeStruct((devices * width, features), jnp.float32),
            jax.ShapeDtypeStruct((2 * blocks, LANES), jnp.int32),
        ),
        in_specs=[hbm, hbm, hbm],
        out_specs=(vmem, vmem),
        scratch_shapes=[
            pltpu.VMEM((blocks, LANES), jnp.int32),
            pltpu.VMEM((block_map.shape[0] // LANES, LANES), jnp.int32),
            pltpu.VMEM((look_count, features), jnp.float32),
            pltpu.VMEM((look_count, LANES), jnp.int32),
            pltpu.VMEM((look_count, LANES), jnp.int32),
            pltpu.VMEM((blocks, LANES), jnp.int32),
            pltpu.SMEM((blocks, LANES), jnp.int32),
            [pltpu.VMEM((devices * width + 8, features), jnp.float32)] * STREAMS,
            pltpu.SemaphoreType.DMA((4,)),
        ],
        compiler_params=pltpu.CompilerParams(vmem_limit_bytes=24 << 20),
        name="bin_rows",
    )(row_ids.reshape(blocks, LANES), block_map.reshape(-1, LANES), grad_tiles)

    got = lax.all_to_all(send, axes, split_axis=0, concat_axis=0, tiled=True)
    guests = got.reshape(devices, width, features)[:, width - guest_width :, :]
    guests = lax.ppermute(guests, "gx", [(i, i ^ 1) for i in range(lax.axis_size("gx"))])
    guests = guests.reshape(devices * guest_width, features)

    def apply_step(rounds, *args):
        new_table, new_accum = pl.pallas_call(
            functools.partial(update_kernel, devices, rounds),
            out_shape=(
                jax.ShapeDtypeStruct(table.shape, jnp.float32),
                jax.ShapeDtypeStruct((rows_dev // LANES, LANES), jnp.float32),
            ),
            in_specs=[vmem] * (2 * rounds + 1) + [hbm],
            out_specs=(hbm, vmem),
            scratch_shapes=[
                pltpu.VMEM((rows_dev + 8, features), jnp.float32),
                pltpu.VMEM((rows_dev, features), jnp.float32),
                pltpu.VMEM(((rounds + 1) * devices, LANES), jnp.int32),
                pltpu.SMEM(((rounds + 1) * devices, LANES), jnp.int32),
                pltpu.SemaphoreType.DMA((CHUNKS,)),
                pltpu.SemaphoreType.DMA((CHUNKS,)),
                pltpu.SemaphoreType.DMA(()),
            ],
            compiler_params=pltpu.CompilerParams(vmem_limit_bytes=24 << 20),
            name=f"apply_step_{rounds}",
        )(*args, got, guests, accum.reshape(-1, LANES), table)
        return new_table, new_accum.reshape(-1)

    def two_rounds():
        mark, position = info[:blocks].reshape(-1), info[blocks:].reshape(-1)
        owner, slot = position // rows_dev, position % rows_dev
        limit = devices * more_slots
        left = mark >= devices * LANES
        lookup = jnp.arange(look_count, dtype=jnp.int32)
        same = left[:, None] & left[None, :] & (position[:, None] == position[None, :])
        first = jnp.min(jnp.where(same, lookup[None, :], look_count), axis=1)
        lead = left & (first == lookup)
        before = lead[None, :] & (owner[:, None] == owner[None, :]) & (lookup[None, :] < first[:, None])
        rank = jnp.sum(before.astype(jnp.int32), axis=1)
        at = jnp.where(left, owner * more_slots + rank, limit)
        rows = jnp.zeros((limit, features), jnp.float32).at[at].add(grad_tiles, mode="drop")
        places = jnp.full((limit,), rows_dev, jnp.int32).at[at].set(slot, mode="drop")
        rows = lax.all_to_all(rows, axes, split_axis=0, concat_axis=0, tiled=True)
        places = lax.all_to_all(places, axes, split_axis=0, concat_axis=0, tiled=True)
        places = places.reshape(devices, more_slots)
        count = jnp.sum((places < rows_dev).astype(jnp.int32), axis=1, keepdims=True)
        places = jnp.pad(places, ((0, 0), (0, LANES - 1 - more_slots)), constant_values=rows_dev)
        return apply_step(2, jnp.concatenate([places, count], axis=1), rows)

    over = jnp.max(got.reshape(devices, width, features)[:, slots, LANES - 2]) > 0.5
    return lax.cond(over, two_rounds, lambda: apply_step(1))


def solution(mesh):
    in_specs = (P(("gx", "gy")), P(), P(("gx", "gy"), None), P(("gx", "gy"), None), P(("gx", "gy")))
    out_specs = (P(("gx", "gy"), None), P(("gx", "gy")))
    return jax.shard_map(
        on_device, mesh=mesh, in_specs=in_specs, out_specs=out_specs, check_vma=False
    )
```

```python
import functools

import jax
import jax.numpy as jnp
from jax import lax
from jax.experimental import pallas as pl
from jax.experimental.pallas import tpu as pltpu
from jax.sharding import PartitionSpec as P

BLOCK = 128
LANES = 128
STREAMS = 8
GROUP = 8
BATCH = 16
CHUNKS = 8

learning_rate = 0.25
epsilon = 1e-08


def split(x, n):
    if n & (n - 1) == 0:
        return lax.shift_right_logical(x, n.bit_length() - 1), x & (n - 1)
    return lax.div(x, n), lax.rem(x, n)


def bin_kernel(
    devices, group, spare, rows_dev, ids_hbm, map_hbm, grad_hbm, send_ref, info_ref, ids_ref, map_ref, grad_ref, cols, marks, target_vmem, target, sums, sems
):
    blocks = ids_ref.shape[0]
    width = send_ref.shape[0] // devices
    slots = width - 1
    drop = devices * width
    fetch = pltpu.make_async_copy(grad_hbm, grad_ref, sems.at[0])
    fetch_ids = pltpu.make_async_copy(ids_hbm, ids_ref, sems.at[1])
    fetch_map = pltpu.make_async_copy(map_hbm, map_ref, sems.at[2])
    fetch_ids.start()
    fetch_map.start()
    fetch.start()
    fetch_ids.wait()
    fetch_map.wait()

    block, within = split(ids_ref[...], BLOCK)
    high, low = split(block, LANES)
    mapped = jnp.zeros_like(block)
    for h in range(map_ref.shape[0]):
        row = jnp.broadcast_to(map_ref[h : h + 1, :], low.shape)
        mapped = jnp.where(high == h, jnp.take_along_axis(row, low, axis=1), mapped)
    position = mapped * BLOCK + within
    owner, slot = split(position, rows_dev)

    def column(row):
        return jnp.transpose(jnp.broadcast_to(row, (LANES, LANES)))

    for b in range(blocks):
        cols[b * LANES : (b + 1) * LANES, :] = column(position[b : b + 1, :])
    rows = [jnp.broadcast_to(position[b : b + 1, :], (8, LANES)) for b in range(blocks)]
    per_block = LANES // 8
    none = blocks * per_block
    first = [jnp.full((8, LANES), none, jnp.int32) for _ in range(blocks)]
    for v in reversed(range(blocks * per_block)):
        col = cols[8 * v : 8 * v + 8, :]
        for b in range(v // per_block, blocks):
            first[b] = jnp.where(col == rows[b], v, first[b])
    sublane = lax.broadcasted_iota(jnp.int32, (8, LANES), 0)
    lane = lax.broadcasted_iota(jnp.int32, (1, LANES), 1)
    leads = [
        jnp.min(first[b] * 8 + sublane, axis=0, keepdims=True) == lane + b * LANES for b in range(blocks)
    ]

    device = lax.broadcasted_iota(jnp.int32, (devices, LANES), 0)
    owned = [device == owner[b : b + 1, :] for b in range(blocks)]
    hot = [owned[b] & leads[b] for b in range(blocks)]
    hot16 = jnp.concatenate([h.astype(jnp.float32) for h in hot], axis=0).astype(jnp.bfloat16)
    i0 = lax.broadcasted_iota(jnp.int32, (LANES, 2 * LANES), 0)
    i1 = lax.broadcasted_iota(jnp.int32, (LANES, 2 * LANES), 1)
    ahead = ((i0 < i1)).astype(jnp.float32).astype(jnp.bfloat16)
    counted = jnp.dot(hot16, ahead, preferred_element_type=jnp.float32)
    counts = jnp.zeros((devices, LANES), jnp.float32)
    ranks = []
    for b in range(blocks):
        here = counted[b * devices : (b + 1) * devices]
        ranks.append(jnp.sum(jnp.where(owned[b], here[:, :LANES] + counts, 0.0), axis=0, keepdims=True))
        counts = counts + here[:, LANES:]

    def partner(x):
        parts = [x[i : i + group] for i in range(0, devices, group)]
        return jnp.concatenate([parts[i ^ 1] for i in range(len(parts))], axis=0)

    kept = jnp.minimum(counts, slots)
    extra = counts - kept
    fits = (extra <= spare) & (partner(kept) + extra <= slots)
    shift = jnp.where(fits, slots - counts, -2.0 * LANES)
    guests = partner(jnp.where(fits, extra, 0.0))

    header_high = jnp.zeros((devices, LANES), jnp.float32)
    header_low = jnp.zeros((devices, LANES), jnp.float32)
    slot_high, slot_low = split(slot, LANES)
    lanes = lax.broadcasted_iota(jnp.int32, (LANES, LANES), 1)
    nowhere = devices * LANES
    for b in range(blocks):
        moved = ranks[b] + jnp.sum(jnp.where(owned[b], shift, 0.0), axis=0, keepdims=True)
        at_home = ranks[b] < slots
        mine = owner[b : b + 1, :]
        across, _ = split(mine, group)
        other = mine + jnp.where((across & 1) == 0, group, -group)
        bin_of = jnp.where(at_home, mine, jnp.where(moved >= 0.0, other, devices))
        row_of = jnp.where(at_home, ranks[b], jnp.where(moved >= 0.0, moved, 0.0)).astype(jnp.int32)
        bin_of = jnp.where(leads[b], bin_of, devices)
        mark_col = column(jnp.where(bin_of < devices, bin_of * LANES + row_of, nowhere))
        marks[b * LANES : (b + 1) * LANES, :] = mark_col
        place = ((mark_col & (LANES - 1)) == lanes).astype(jnp.float32).astype(jnp.bfloat16)
        sent = device == bin_of
        both = jnp.concatenate(
            [
                jnp.where(sent, slot_high[b : b + 1, :].astype(jnp.float32), 0.0),
                jnp.where(sent, slot_low[b : b + 1, :].astype(jnp.float32), 0.0),
            ],
            axis=0,
        ).astype(jnp.bfloat16)
        parts = jnp.dot(both, place, preferred_element_type=jnp.float32)
        header_high = header_high + parts[:devices]
        header_low = header_low + parts[devices:]

    best = [jnp.full((8, LANES), nowhere, jnp.int32) for _ in range(blocks)]
    for v in reversed(range(blocks * per_block)):
        col = cols[8 * v : 8 * v + 8, :]
        mark = marks[8 * v : 8 * v + 8, :]
        for b in range(v // per_block, blocks):
            best[b] = jnp.where(col == rows[b], jnp.minimum(mark, best[b]), best[b])
    mark = jnp.concatenate([jnp.min(x, axis=0, keepdims=True) for x in best], axis=0)
    target_vmem[...] = jnp.where(
        mark < nowhere, lax.shift_right_logical(mark, 7) * width + (mark & (LANES - 1)), drop
    )
    send_target = pltpu.make_async_copy(target_vmem, target, sems.at[3])
    send_target.start()
    info_ref[0:blocks, :] = mark
    info_ref[blocks : 2 * blocks, :] = position

    for s in range(STREAMS):
        sums[s][...] = jnp.zeros_like(sums[s])
    over = jnp.max(jnp.where(fits, 0.0, 1.0))
    header = header_high * LANES + header_low
    header = jnp.where(lane == LANES - 1, kept, header)
    header = jnp.where(lane == LANES - 2, over, header)
    header = jnp.where(lane == LANES - 3, guests, header)
    send_target.wait()
    fetch.wait()

    @pl.loop(0, blocks)
    def _(b):
        for c0 in range(0, LANES, STREAMS):
            at = [target[b, c0 + s] for s in range(STREAMS)]
            old = [sums[s][pl.ds(at[s], 1), :] for s in range(STREAMS)]
            new = [old[s] + grad_ref[pl.ds(b * LANES + c0 + s, 1), :] for s in range(STREAMS)]
            for s in range(STREAMS):
                sums[s][pl.ds(at[s], 1), :] = new[s]

    total = sums[0][0:drop, :]
    for s in range(1, STREAMS):
        total = total + sums[s][0:drop, :]
    send_ref[...] = total
    send_ref[pl.ds(slots, devices, stride=width), :] = header


def update_kernel(
    devices, rounds, *refs
):
    if rounds == 2:
        more_head_ref, more_ref, *refs = refs
    got_ref, guest_ref, accum_ref, table_hbm, table_out, accum_out, sums, table, head_vmem, head, sems_in, sems_out, sem = refs
    width = got_ref.shape[0] // devices
    slots = width - 1
    rows_dev = table.shape[0]
    chunk = rows_dev // CHUNKS
    guest_width = guest_ref.shape[0] // devices
    lane = lax.broadcasted_iota(jnp.int32, (devices, LANES), 1)
    last = LANES - 1
    own = got_ref[pl.ds(slots, devices, stride=width), :].astype(jnp.int32)
    head_vmem[0:devices, :] = jnp.where((lane < own[:, last:]) | (lane == last), own, rows_dev)
    guest = guest_ref[pl.ds(guest_width - 1, devices, stride=guest_width), :].astype(jnp.int32)
    guests = guest[:, last - 2 : last - 1]
    head_vmem[devices : 2 * devices, :] = jnp.where(
        lane == last, guests, jnp.where((lane >= slots - guests) & (lane < slots), guest, rows_dev)
    )
    if rounds == 2:
        head_vmem[2 * devices : 3 * devices, :] = more_head_ref[...]
    load_head = pltpu.make_async_copy(head_vmem, head, sem)
    load_head.start()
    loads = [
        pltpu.make_async_copy(
            table_hbm.at[pl.ds(c * chunk, chunk), :], table.at[pl.ds(c * chunk, chunk), :], sems_in.at[c]
        )
        for c in range(CHUNKS)
    ]
    for load in loads:
        load.start()
    for k in range(2):
        sums[k][...] = jnp.zeros_like(sums[k])
    load_head.wait()

    def add_pair(section, d, c0, rows_ref, first, step, size):
        spots = [[head[section * devices + d + k, c0 + u] for u in range(size)] for k in range(2)]
        plan = [(k, u) for u in range(0, size, GROUP) for k in range(2)]
        late = []
        for k, u0 in plan:
            now = []
            for u in range(u0, min(u0 + GROUP, size)):
                here = pl.ds(spots[k][u], 1)
                now.append((k, here, sums[k][here, :] + rows_ref[pl.ds(first + k * step + u, 1), :]))
                if late:
                    j, there, value = late.pop(0)
                    sums[j][there, :] = value
            for j, there, value in late:
                sums[j][there, :] = value
            late = now
        for j, there, value in late:
            sums[j][there, :] = value

    def add_rows(section, d, rows_ref, width):
        count = jnp.maximum(head[section * devices + d, last], head[section * devices + d + 1, last])
        for r0 in range(0, width, BATCH):

            @pl.when(count > r0)
            def _():
                add_pair(section, d, r0, rows_ref, d * width + r0, width, min(BATCH, width - r0))

    for d in range(0, devices, 2):
        add_rows(0, d, got_ref, width)
        guests = jnp.maximum(head[devices + d, last], head[devices + d + 1, last])
        for r0 in range(guest_width - 8, -1, -8):

            @pl.when(guests > max(guest_width - 9 - r0, 0))
            def _():
                add_pair(1, d, width - guest_width + r0, guest_ref, d * guest_width + r0, guest_width, 8)

    if rounds == 2:
        more_width = more_ref.shape[0] // devices

        @pl.loop(0, devices // 2)
        def _(i):
            add_rows(2, 2 * i, more_ref, more_width)

    groups = chunk // LANES
    stores = []
    for c in range(CHUNKS):
        heres = [pl.ds((c * groups + i) * LANES, LANES) for i in range(groups)]
        these = pl.ds(c * groups, groups)
        squares = [jnp.transpose(jnp.square(sums[0][here, :] + sums[1][here, :])) for here in heres]
        totals = jnp.concatenate([jnp.sum(x, axis=0, keepdims=True) for x in squares], axis=0)
        new_accum = accum_ref[these, :] + totals * (1.0 / LANES)
        accum_out[these, :] = new_accum
        scale = learning_rate / (jnp.sqrt(new_accum) + epsilon)
        loads[c].wait()
        for i, here in enumerate(heres):
            factor = jnp.transpose(jnp.broadcast_to(scale[i : i + 1, :], (LANES, LANES)))
            table[here, :] = table[here, :] - factor * (sums[0][here, :] + sums[1][here, :])

        store = pltpu.make_async_copy(
            table.at[pl.ds(c * chunk, chunk), :], table_out.at[pl.ds(c * chunk, chunk), :], sems_out.at[c]
        )
        store.start()
        stores.append(store)
    for store in stores:
        store.wait()


def on_device(row_ids, block_map, grad_tiles, table, accum):
    axes = ("gx", "gy")
    devices = lax.axis_size("gx") * lax.axis_size("gy")
    rows_dev, features = table.shape
    look_count = row_ids.shape[0]
    capacity = 2 * look_count // devices
    width = -(-capacity * 5 // 8 // 8) * 8
    guest_width = -(-width * 3 // 10 // 8) * 8
    slots = width - 1
    more_slots = -(-(capacity - slots) // 16) * 16
    blocks = look_count // LANES
    vmem = pl.BlockSpec(memory_space=pltpu.VMEM)
    hbm = pl.BlockSpec(memory_space=pltpu.MemorySpace.HBM)

    send, info = pl.pallas_call(
        functools.partial(bin_kernel, devices, lax.axis_size("gy"), guest_width - 1, rows_dev),
        out_shape=(
            jax.ShapeDtypeStruct((devices * width, features), jnp.float32),
            jax.ShapeDtypeStruct((2 * blocks, LANES), jnp.int32),
        ),
        in_specs=[hbm, hbm, hbm],
        out_specs=(vmem, vmem),
        scratch_shapes=[
            pltpu.VMEM((blocks, LANES), jnp.int32),
            pltpu.VMEM((block_map.shape[0] // LANES, LANES), jnp.int32),
            pltpu.VMEM((look_count, features), jnp.float32),
            pltpu.VMEM((look_count, LANES), jnp.int32),
            pltpu.VMEM((look_count, LANES), jnp.int32),
            pltpu.VMEM((blocks, LANES), jnp.int32),
            pltpu.SMEM((blocks, LANES), jnp.int32),
            [pltpu.VMEM((devices * width + 8, features), jnp.float32)] * STREAMS,
            pltpu.SemaphoreType.DMA((4,)),
        ],
        compiler_params=pltpu.CompilerParams(vmem_limit_bytes=24 << 20),
        name="bin_rows",
    )(
        pltpu.with_memory_space_constraint(row_ids.reshape(blocks, LANES), pltpu.HBM),
        pltpu.with_memory_space_constraint(block_map.reshape(-1, LANES), pltpu.HBM),
        grad_tiles,
    )

    got = lax.all_to_all(send, axes, split_axis=0, concat_axis=0, tiled=True)
    guests = got.reshape(devices, width, features)[:, width - guest_width :, :]
    guests = lax.ppermute(guests, "gx", [(i, i ^ 1) for i in range(lax.axis_size("gx"))])
    guests = guests.reshape(devices * guest_width, features)

    def apply_step(rounds, *args):
        new_table, new_accum = pl.pallas_call(
            functools.partial(update_kernel, devices, rounds),
            out_shape=(
                jax.ShapeDtypeStruct(table.shape, jnp.float32),
                jax.ShapeDtypeStruct((rows_dev // LANES, LANES), jnp.float32),
            ),
            in_specs=[vmem] * (2 * rounds + 1) + [hbm],
            out_specs=(hbm, vmem),
            scratch_shapes=[
                [pltpu.VMEM((rows_dev + 8, features), jnp.float32)] * 2,
                pltpu.VMEM((rows_dev, features), jnp.float32),
                pltpu.VMEM(((rounds + 1) * devices, LANES), jnp.int32),
                pltpu.SMEM(((rounds + 1) * devices, LANES), jnp.int32),
                pltpu.SemaphoreType.DMA((CHUNKS,)),
                pltpu.SemaphoreType.DMA((CHUNKS,)),
                pltpu.SemaphoreType.DMA(()),
            ],
            compiler_params=pltpu.CompilerParams(vmem_limit_bytes=24 << 20),
            name=f"apply_step_{rounds}",
        )(*args, got, guests, accum.reshape(-1, LANES), table)
        return new_table, new_accum.reshape(-1)

    def two_rounds():
        mark, position = info[:blocks].reshape(-1), info[blocks:].reshape(-1)
        owner, slot = position // rows_dev, position % rows_dev
        limit = devices * more_slots
        left = mark >= devices * LANES
        lookup = jnp.arange(look_count, dtype=jnp.int32)
        same = left[:, None] & left[None, :] & (position[:, None] == position[None, :])
        first = jnp.min(jnp.where(same, lookup[None, :], look_count), axis=1)
        lead = left & (first == lookup)
        before = lead[None, :] & (owner[:, None] == owner[None, :]) & (lookup[None, :] < first[:, None])
        rank = jnp.sum(before.astype(jnp.int32), axis=1)
        at = jnp.where(left, owner * more_slots + rank, limit)
        rows = jnp.zeros((limit, features), jnp.float32).at[at].add(grad_tiles, mode="drop")
        places = jnp.full((limit,), rows_dev, jnp.int32).at[at].set(slot, mode="drop")
        rows = lax.all_to_all(rows, axes, split_axis=0, concat_axis=0, tiled=True)
        places = lax.all_to_all(places, axes, split_axis=0, concat_axis=0, tiled=True)
        places = places.reshape(devices, more_slots)
        count = jnp.sum((places < rows_dev).astype(jnp.int32), axis=1, keepdims=True)
        places = jnp.pad(places, ((0, 0), (0, LANES - 1 - more_slots)), constant_values=rows_dev)
        return apply_step(2, jnp.concatenate([places, count], axis=1), rows)

    over = jnp.max(got.reshape(devices, width, features)[:, slots, LANES - 2]) > 0.5
    return lax.cond(over, two_rounds, lambda: apply_step(1))


def solution(mesh):
    in_specs = (P(("gx", "gy")), P(), P(("gx", "gy"), None), P(("gx", "gy"), None), P(("gx", "gy")))
    out_specs = (P(("gx", "gy"), None), P(("gx", "gy")))
    return jax.shard_map(
        on_device, mesh=mesh, in_specs=in_specs, out_specs=out_specs, check_vma=False
    )
```

```python
import functools

import jax
import jax.numpy as jnp
from jax import lax
from jax.experimental import pallas as pl
from jax.experimental.pallas import tpu as pltpu
from jax.sharding import PartitionSpec as P

BLOCK = 128
LANES = 128
STREAMS = 8
GROUP = 8
BATCH = 16
CHUNKS = 4

learning_rate = 0.25
epsilon = 1e-08


def split(x, n):
    if n & (n - 1) == 0:
        return lax.shift_right_logical(x, n.bit_length() - 1), x & (n - 1)
    return lax.div(x, n), lax.rem(x, n)


def bin_kernel(
    devices, group, spare, rows_dev, ids_hbm, map_hbm, grad_hbm, send_ref, info_ref, ids_ref, map_ref, grad_ref, cols, marks, target_vmem, target, sums, sems
):
    blocks = ids_ref.shape[0]
    width = send_ref.shape[0] // devices
    slots = width - 1
    drop = devices * width
    fetch = pltpu.make_async_copy(grad_hbm, grad_ref, sems.at[0])
    fetch_ids = pltpu.make_async_copy(ids_hbm, ids_ref, sems.at[1])
    fetch_map = pltpu.make_async_copy(map_hbm, map_ref, sems.at[2])
    fetch_ids.start()
    fetch_map.start()
    fetch.start()
    fetch_ids.wait()
    fetch_map.wait()

    block, within = split(ids_ref[...], BLOCK)
    high, low = split(block, LANES)
    mapped = jnp.zeros_like(block)
    for h in range(map_ref.shape[0]):
        row = jnp.broadcast_to(map_ref[h : h + 1, :], low.shape)
        mapped = jnp.where(high == h, jnp.take_along_axis(row, low, axis=1), mapped)
    position = mapped * BLOCK + within
    owner, slot = split(position, rows_dev)

    def column(row):
        return jnp.transpose(jnp.broadcast_to(row, (LANES, LANES)))

    for b in range(blocks):
        cols[b * LANES : (b + 1) * LANES, :] = column(position[b : b + 1, :])
    rows = [jnp.broadcast_to(position[b : b + 1, :], (8, LANES)) for b in range(blocks)]
    per_block = LANES // 8
    none = blocks * per_block
    first = [jnp.full((8, LANES), none, jnp.int32) for _ in range(blocks)]
    for v in reversed(range(blocks * per_block)):
        col = cols[8 * v : 8 * v + 8, :]
        for b in range(v // per_block, blocks):
            first[b] = jnp.where(col == rows[b], v, first[b])
    sublane = lax.broadcasted_iota(jnp.int32, (8, LANES), 0)
    lane = lax.broadcasted_iota(jnp.int32, (1, LANES), 1)
    leads = [
        jnp.min(first[b] * 8 + sublane, axis=0, keepdims=True) == lane + b * LANES for b in range(blocks)
    ]

    device = lax.broadcasted_iota(jnp.int32, (devices, LANES), 0)
    owned = [device == owner[b : b + 1, :] for b in range(blocks)]
    hot = [owned[b] & leads[b] for b in range(blocks)]
    hot16 = jnp.concatenate([h.astype(jnp.float32) for h in hot], axis=0).astype(jnp.bfloat16)
    i0 = lax.broadcasted_iota(jnp.int32, (LANES, 2 * LANES), 0)
    i1 = lax.broadcasted_iota(jnp.int32, (LANES, 2 * LANES), 1)
    ahead = ((i0 < i1)).astype(jnp.float32).astype(jnp.bfloat16)
    counted = jnp.dot(hot16, ahead, preferred_element_type=jnp.float32)
    counts = jnp.zeros((devices, LANES), jnp.float32)
    ranks = []
    for b in range(blocks):
        here = counted[b * devices : (b + 1) * devices]
        ranks.append(jnp.sum(jnp.where(owned[b], here[:, :LANES] + counts, 0.0), axis=0, keepdims=True))
        counts = counts + here[:, LANES:]

    def partner(x):
        parts = [x[i : i + group] for i in range(0, devices, group)]
        return jnp.concatenate([parts[i ^ 1] for i in range(len(parts))], axis=0)

    kept = jnp.minimum(counts, slots)
    extra = counts - kept
    fits = (extra <= spare) & (partner(kept) + extra <= slots)
    shift = jnp.where(fits, slots - counts, -2.0 * LANES)
    guests = partner(jnp.where(fits, extra, 0.0))

    header_high = jnp.zeros((devices, LANES), jnp.float32)
    header_low = jnp.zeros((devices, LANES), jnp.float32)
    slot_high, slot_low = split(slot, LANES)
    lanes = lax.broadcasted_iota(jnp.int32, (LANES, LANES), 1)
    nowhere = devices * LANES
    for b in range(blocks):
        moved = ranks[b] + jnp.sum(jnp.where(owned[b], shift, 0.0), axis=0, keepdims=True)
        at_home = ranks[b] < slots
        mine = owner[b : b + 1, :]
        across, _ = split(mine, group)
        other = mine + jnp.where((across & 1) == 0, group, -group)
        bin_of = jnp.where(at_home, mine, jnp.where(moved >= 0.0, other, devices))
        row_of = jnp.where(at_home, ranks[b], jnp.where(moved >= 0.0, moved, 0.0)).astype(jnp.int32)
        bin_of = jnp.where(leads[b], bin_of, devices)
        mark_col = column(jnp.where(bin_of < devices, bin_of * LANES + row_of, nowhere))
        marks[b * LANES : (b + 1) * LANES, :] = mark_col
        place = ((mark_col & (LANES - 1)) == lanes).astype(jnp.float32).astype(jnp.bfloat16)
        sent = device == bin_of
        both = jnp.concatenate(
            [
                jnp.where(sent, slot_high[b : b + 1, :].astype(jnp.float32), 0.0),
                jnp.where(sent, slot_low[b : b + 1, :].astype(jnp.float32), 0.0),
            ],
            axis=0,
        ).astype(jnp.bfloat16)
        parts = jnp.dot(both, place, preferred_element_type=jnp.float32)
        header_high = header_high + parts[:devices]
        header_low = header_low + parts[devices:]

    best = [jnp.full((8, LANES), nowhere, jnp.int32) for _ in range(blocks)]
    for v in reversed(range(blocks * per_block)):
        col = cols[8 * v : 8 * v + 8, :]
        mark = marks[8 * v : 8 * v + 8, :]
        for b in range(v // per_block, blocks):
            best[b] = jnp.where(col == rows[b], jnp.minimum(mark, best[b]), best[b])
    mark = jnp.concatenate([jnp.min(x, axis=0, keepdims=True) for x in best], axis=0)
    target_vmem[...] = jnp.where(
        mark < nowhere, lax.shift_right_logical(mark, 7) * width + (mark & (LANES - 1)), drop
    )
    send_target = pltpu.make_async_copy(target_vmem, target, sems.at[3])
    send_target.start()
    info_ref[0:blocks, :] = mark
    info_ref[blocks : 2 * blocks, :] = position

    for s in range(STREAMS):
        sums[s][...] = jnp.zeros_like(sums[s])
    over = jnp.max(jnp.where(fits, 0.0, 1.0))
    header = header_high * LANES + header_low
    header = jnp.where(lane == LANES - 1, kept, header)
    header = jnp.where(lane == LANES - 2, over, header)
    header = jnp.where(lane == LANES - 3, guests, header)
    send_target.wait()
    fetch.wait()

    @pl.loop(0, blocks)
    def _(b):
        for c0 in range(0, LANES, STREAMS):
            at = [target[b, c0 + s] for s in range(STREAMS)]
            old = [sums[s][pl.ds(at[s], 1), :] for s in range(STREAMS)]
            new = [old[s] + grad_ref[pl.ds(b * LANES + c0 + s, 1), :] for s in range(STREAMS)]
            for s in range(STREAMS):
                sums[s][pl.ds(at[s], 1), :] = new[s]

    total = sums[0][0:drop, :]
    for s in range(1, STREAMS):
        total = total + sums[s][0:drop, :]
    send_ref[...] = total
    send_ref[pl.ds(slots, devices, stride=width), :] = header


def update_kernel(
    devices, rounds, *refs
):
    if rounds == 2:
        more_head_ref, more_ref, *refs = refs
    got_ref, guest_ref, accum_ref, table_hbm, table_out, accum_out, sums, table, head_vmem, head, sems_in, sems_out, sem = refs
    width = got_ref.shape[0] // devices
    slots = width - 1
    rows_dev = table.shape[0]
    chunk = rows_dev // CHUNKS
    guest_width = guest_ref.shape[0] // devices
    lane = lax.broadcasted_iota(jnp.int32, (devices, LANES), 1)
    last = LANES - 1
    own = got_ref[pl.ds(slots, devices, stride=width), :].astype(jnp.int32)
    head_vmem[0:devices, :] = jnp.where((lane < own[:, last:]) | (lane == last), own, rows_dev)
    guest = guest_ref[pl.ds(guest_width - 1, devices, stride=guest_width), :].astype(jnp.int32)
    guests = guest[:, last - 2 : last - 1]
    head_vmem[devices : 2 * devices, :] = jnp.where(
        lane == last, guests, jnp.where((lane >= slots - guests) & (lane < slots), guest, rows_dev)
    )
    if rounds == 2:
        head_vmem[2 * devices : 3 * devices, :] = more_head_ref[...]
    load_head = pltpu.make_async_copy(head_vmem, head, sem)
    load_head.start()
    loads = [
        pltpu.make_async_copy(
            table_hbm.at[pl.ds(c * chunk, chunk), :], table.at[pl.ds(c * chunk, chunk), :], sems_in.at[c]
        )
        for c in range(CHUNKS)
    ]
    for load in loads:
        load.start()
    for k in range(2):
        sums[k][...] = jnp.zeros_like(sums[k])
    load_head.wait()

    def add_pair(section, d, c0, rows_ref, first, step, size):
        spots = [[head[section * devices + d + k, c0 + u] for u in range(size)] for k in range(2)]
        plan = [(k, u) for u in range(0, size, GROUP) for k in range(2)]
        late = []
        for k, u0 in plan:
            now = []
            for u in range(u0, min(u0 + GROUP, size)):
                here = pl.ds(spots[k][u], 1)
                now.append((k, here, sums[k][here, :] + rows_ref[pl.ds(first + k * step + u, 1), :]))
                if late:
                    j, there, value = late.pop(0)
                    sums[j][there, :] = value
            for j, there, value in late:
                sums[j][there, :] = value
            late = now
        for j, there, value in late:
            sums[j][there, :] = value

    def add_rows(section, d, rows_ref, width):
        count = jnp.maximum(head[section * devices + d, last], head[section * devices + d + 1, last])
        for r0 in range(0, width, BATCH):

            @pl.when(count > r0)
            def _():
                add_pair(section, d, r0, rows_ref, d * width + r0, width, min(BATCH, width - r0))

    for d in range(0, devices, 2):
        add_rows(0, d, got_ref, width)
        guests = jnp.maximum(head[devices + d, last], head[devices + d + 1, last])
        for r0 in range(guest_width - 8, -1, -8):

            @pl.when(guests > max(guest_width - 9 - r0, 0))
            def _():
                add_pair(1, d, width - guest_width + r0, guest_ref, d * guest_width + r0, guest_width, 8)

    if rounds == 2:
        more_width = more_ref.shape[0] // devices

        @pl.loop(0, devices // 2)
        def _(i):
            add_rows(2, 2 * i, more_ref, more_width)

    groups = chunk // LANES
    scales = []
    for c in range(CHUNKS):
        heres = [pl.ds((c * groups + i) * LANES, LANES) for i in range(groups)]
        these = pl.ds(c * groups, groups)
        squares = [jnp.transpose(jnp.square(sums[0][here, :] + sums[1][here, :])) for here in heres]
        totals = jnp.concatenate([jnp.sum(x, axis=0, keepdims=True) for x in squares], axis=0)
        new_accum = accum_ref[these, :] + totals * (1.0 / LANES)
        accum_out[these, :] = new_accum
        scales.append(learning_rate / (jnp.sqrt(new_accum) + epsilon))

    stores = []
    for c in range(CHUNKS):
        loads[c].wait()
        for i in range(groups):
            here = pl.ds((c * groups + i) * LANES, LANES)
            factor = jnp.transpose(jnp.broadcast_to(scales[c][i : i + 1, :], (LANES, LANES)))
            table[here, :] = table[here, :] - factor * (sums[0][here, :] + sums[1][here, :])

        store = pltpu.make_async_copy(
            table.at[pl.ds(c * chunk, chunk), :], table_out.at[pl.ds(c * chunk, chunk), :], sems_out.at[c]
        )
        store.start()
        stores.append(store)
    for store in stores:
        store.wait()


def on_device(row_ids, block_map, grad_tiles, table, accum):
    axes = ("gx", "gy")
    devices = lax.axis_size("gx") * lax.axis_size("gy")
    rows_dev, features = table.shape
    look_count = row_ids.shape[0]
    capacity = 2 * look_count // devices
    width = -(-capacity * 5 // 8 // 8) * 8
    guest_width = -(-width * 3 // 10 // 8) * 8
    slots = width - 1
    more_slots = -(-(capacity - slots) // 16) * 16
    blocks = look_count // LANES
    vmem = pl.BlockSpec(memory_space=pltpu.VMEM)
    hbm = pl.BlockSpec(memory_space=pltpu.MemorySpace.HBM)

    send, info = pl.pallas_call(
        functools.partial(bin_kernel, devices, lax.axis_size("gy"), guest_width - 1, rows_dev),
        out_shape=(
            jax.ShapeDtypeStruct((devices * width, features), jnp.float32),
            jax.ShapeDtypeStruct((2 * blocks, LANES), jnp.int32),
        ),
        in_specs=[hbm, hbm, hbm],
        out_specs=(vmem, vmem),
        scratch_shapes=[
            pltpu.VMEM((blocks, LANES), jnp.int32),
            pltpu.VMEM((block_map.shape[0] // LANES, LANES), jnp.int32),
            pltpu.VMEM((look_count, features), jnp.float32),
            pltpu.VMEM((look_count, LANES), jnp.int32),
            pltpu.VMEM((look_count, LANES), jnp.int32),
            pltpu.VMEM((blocks, LANES), jnp.int32),
            pltpu.SMEM((blocks, LANES), jnp.int32),
            [pltpu.VMEM((devices * width + 8, features), jnp.float32)] * STREAMS,
            pltpu.SemaphoreType.DMA((4,)),
        ],
        compiler_params=pltpu.CompilerParams(vmem_limit_bytes=24 << 20),
        name="bin_rows",
    )(
        pltpu.with_memory_space_constraint(row_ids.reshape(blocks, LANES), pltpu.HBM),
        pltpu.with_memory_space_constraint(block_map.reshape(-1, LANES), pltpu.HBM),
        grad_tiles,
    )

    got = lax.all_to_all(send, axes, split_axis=0, concat_axis=0, tiled=True)
    guests = got.reshape(devices, width, features)[:, width - guest_width :, :]
    guests = lax.ppermute(guests, "gx", [(i, i ^ 1) for i in range(lax.axis_size("gx"))])
    guests = guests.reshape(devices * guest_width, features)

    def apply_step(rounds, *args):
        new_table, new_accum = pl.pallas_call(
            functools.partial(update_kernel, devices, rounds),
            out_shape=(
                jax.ShapeDtypeStruct(table.shape, jnp.float32),
                jax.ShapeDtypeStruct((rows_dev // LANES, LANES), jnp.float32),
            ),
            in_specs=[vmem] * (2 * rounds + 1) + [hbm],
            out_specs=(hbm, vmem),
            scratch_shapes=[
                [pltpu.VMEM((rows_dev + 8, features), jnp.float32)] * 2,
                pltpu.VMEM((rows_dev, features), jnp.float32),
                pltpu.VMEM(((rounds + 1) * devices, LANES), jnp.int32),
                pltpu.SMEM(((rounds + 1) * devices, LANES), jnp.int32),
                pltpu.SemaphoreType.DMA((CHUNKS,)),
                pltpu.SemaphoreType.DMA((CHUNKS,)),
                pltpu.SemaphoreType.DMA(()),
            ],
            compiler_params=pltpu.CompilerParams(vmem_limit_bytes=24 << 20),
            name=f"apply_step_{rounds}",
        )(*args, got, guests, accum.reshape(-1, LANES), table)
        return new_table, new_accum.reshape(-1)

    def two_rounds():
        mark, position = info[:blocks].reshape(-1), info[blocks:].reshape(-1)
        owner, slot = position // rows_dev, position % rows_dev
        limit = devices * more_slots
        left = mark >= devices * LANES
        lookup = jnp.arange(look_count, dtype=jnp.int32)
        same = left[:, None] & left[None, :] & (position[:, None] == position[None, :])
        first = jnp.min(jnp.where(same, lookup[None, :], look_count), axis=1)
        lead = left & (first == lookup)
        before = lead[None, :] & (owner[:, None] == owner[None, :]) & (lookup[None, :] < first[:, None])
        rank = jnp.sum(before.astype(jnp.int32), axis=1)
        at = jnp.where(left, owner * more_slots + rank, limit)
        rows = jnp.zeros((limit, features), jnp.float32).at[at].add(grad_tiles, mode="drop")
        places = jnp.full((limit,), rows_dev, jnp.int32).at[at].set(slot, mode="drop")
        rows = lax.all_to_all(rows, axes, split_axis=0, concat_axis=0, tiled=True)
        places = lax.all_to_all(places, axes, split_axis=0, concat_axis=0, tiled=True)
        places = places.reshape(devices, more_slots)
        count = jnp.sum((places < rows_dev).astype(jnp.int32), axis=1, keepdims=True)
        places = jnp.pad(places, ((0, 0), (0, LANES - 1 - more_slots)), constant_values=rows_dev)
        return apply_step(2, jnp.concatenate([places, count], axis=1), rows)

    over = jnp.max(got.reshape(devices, width, features)[:, slots, LANES - 2]) > 0.5
    return lax.cond(over, two_rounds, lambda: apply_step(1))


def solution(mesh):
    in_specs = (P(("gx", "gy")), P(), P(("gx", "gy"), None), P(("gx", "gy"), None), P(("gx", "gy")))
    out_specs = (P(("gx", "gy"), None), P(("gx", "gy")))
    return jax.shard_map(
        on_device, mesh=mesh, in_specs=in_specs, out_specs=out_specs, check_vma=False
    )
```
